128 devices in a mesh: chan: 2 (over x_hi), blk: 64 (over y, z, x_lo, core).
Axes of the slice: x: 4 (x_hi: 2, x_lo: 2; x = x_hi * 2 + x_lo), y: 4, z: 4, core: 2. Of those that a mesh axis runs over, the one named last changes fastest.
Arguments:
- features: bfloat16 [64, 2, 256, 128], P('blk', 'chan'), may hold values from -6 to 6
- transforms: bfloat16 [8, 128, 128], replicated, may hold values from -0.5 to 0.5
- self_weight: bfloat16 [128, 128], replicated, may hold values from -0.5 to 0.5
- tile_rows: int32 [8, 64, 64, 8], P('chan', 'blk'), may hold values from 0 to 3
- tile_cols: int32 [8, 64, 64, 8], P('chan', 'blk'), may hold values from 0 to 3
- tile_ids: int32 [8, 64, 64, 8], P('chan', 'blk'), may hold values from 0 to 31
- tile_count: int32 [8, 64, 64], P('chan', 'blk'), may hold values from 0 to 8
- tile_pool: bfloat16 [8, 64, 32, 128, 128], P('chan', 'blk'), may hold values from -0.0234375 to 0.0234375
Outputs:
- updated: bfloat16 [64, 2, 256, 128], P('blk', 'chan')
The draws below stay inside these ranges and needn't reach their ends.
All inputs are finite; a program needn't handle non-finite values.
Results may differ from the reference program's by a relative error of at most 0.0041.
Values may be sent and summed in bfloat16 or wider, within the bound.
No kernel may reach another device: no remote copies, remote signals or barrier semaphores. Data moves between devices by JAX's collectives and lax.ppermute only.
A program may use at most 128 MiB of HBM per device.

```python
import jax
import jax.numpy as jnp
from jax import lax

D = 128
RELS = 8
TILE = 128
TPB = 4
SLOTS = 8
POOL = 32
BLOCKS = 64
HALF = 256
NODES = 32768
N_CHAN = 2


def place_ends(array, key, low, top_value):
    index_at = [jax.random.randint(jax.random.fold_in(key, axis), (), 0, length) for axis, length in enumerate(array.shape)]
    widest = array.shape.index(max(array.shape))
    next_to = index_at[:widest] + [(index_at[widest] + 1) % array.shape[widest]] + index_at[widest + 1:]
    return array.at[tuple(index_at)].set(low).at[tuple(next_to)].set(top_value)


def block_scale(key, shape, shards, least, top_value):
    factor_of, own = 1.0, jax.random.fold_in(key, 6)
    for position, parts in shards:
        draws = jnp.exp(jax.random.uniform(jax.random.fold_in(own, position), (parts,), jnp.float32, least / len(shards), top_value / len(shards)))
        factor_of = factor_of * jnp.repeat(draws, shape[position] // parts).reshape([-1 if axis == position else 1 for axis in range(len(shape))])
    return factor_of


def gaussian(rng, dims, deviation, most, shards=(), held_as=jnp.bfloat16):
    loudness = block_scale(rng, dims, shards, -0.22, 0.18) if shards else 1.0
    array = jax.random.normal(rng, dims, jnp.float32) * deviation * loudness
    return jnp.minimum(jnp.maximum(array, -most), most).astype(held_as)


def setup_inputs(seed: int = 0) -> dict:
    splits = jax.random.split(jax.random.key(seed), 9)
    return {
        "features": gaussian(splits[0], (BLOCKS, N_CHAN, HALF, D), 1.0, 6.0, ((0, 64), (1, 2))),
        "transforms": gaussian(splits[1], (RELS, D, D), D ** -0.5, 0.5),
        "self_weight": gaussian(splits[2], (D, D), D ** -0.5, 0.5),
        "tile_rows": place_ends(jax.random.randint(splits[3], (RELS, BLOCKS, BLOCKS, SLOTS), 0, TPB), jax.random.fold_in(splits[3], 1), 0, TPB - 1).astype(jnp.int32),
        "tile_cols": place_ends(jax.random.randint(splits[4], (RELS, BLOCKS, BLOCKS, SLOTS), 0, TPB), jax.random.fold_in(splits[4], 1), 0, TPB - 1).astype(jnp.int32),
        "tile_ids": place_ends(jax.random.randint(splits[5], (RELS, BLOCKS, BLOCKS, SLOTS), 0, POOL), jax.random.fold_in(splits[5], 1), 0, POOL - 1).astype(jnp.int32),
        "tile_count": place_ends(jax.random.randint(splits[6], (RELS, BLOCKS, BLOCKS), 0, SLOTS + 1), jax.random.fold_in(splits[6], 1), 0, SLOTS).astype(jnp.int32),
        "tile_pool": gaussian(splits[7], (RELS, BLOCKS, POOL, TILE, TILE), (1.0 / (TILE * RELS * BLOCKS * SLOTS / (2 * TPB)) ** 0.5), 0.0234375, ((0, 2), (1, 64))),
    }


def reference(features, transforms, self_weight, tile_rows, tile_cols, tile_ids, tile_count, tile_pool):
    rows_all = features.reshape(NODES, D)
    slot_range = jnp.arange(SLOTS)
    tile_range = jnp.arange(TPB)
    block_range = jnp.arange(BLOCKS)
    agg = jnp.zeros((BLOCKS, TPB, TILE, D), jnp.float32)
    for rel in range(RELS):
        hidden = jnp.dot(rows_all, transforms[rel], preferred_element_type=jnp.float32).astype(jnp.bfloat16)
        hidden = hidden.reshape(BLOCKS, TPB, TILE, D)

        def per_block(dest):
            rows_here = tile_rows[rel, dest]
            cols_here = tile_cols[rel, dest]
            ids_here = tile_ids[rel, dest]
            count_here = tile_count[rel, dest]
            source = hidden[block_range[:, None], cols_here].astype(jnp.float32)
            weights = tile_pool[rel, dest][ids_here].astype(jnp.float32)
            product = jnp.einsum("jkab,jkbd->jkad", weights, source, precision=lax.Precision.HIGHEST)
            live = (slot_range[None, :] < count_here[:, None]).astype(jnp.float32)
            onehot = (rows_here[:, :, None] == tile_range[None, None, :]).astype(jnp.float32) * live[:, :, None]
            return jnp.einsum("jkt,jkad->tad", onehot, product, precision=lax.Precision.HIGHEST)

        agg = agg + lax.map(per_block, block_range)
    selfterm = jnp.dot(rows_all, self_weight, preferred_element_type=jnp.float32)
    updated = jax.nn.relu(selfterm + agg.reshape(NODES, D)).astype(jnp.bfloat16)
    return updated.reshape(BLOCKS, N_CHAN, HALF, D)
```

```python
import functools

import jax
import jax.numpy as jnp
from jax import lax
from jax.experimental import pallas as pl
from jax.experimental.pallas import tpu as pltpu
from jax.sharding import Mesh, PartitionSpec as P

SIDE = 4
TILE = 128
RELS = 4
POOL = 32
TPB = 4
SLOTS = 8
BLOCKS = 64
ZERO = RELS * POOL
UNIT = 4
WIDE = (16, 16, 8, 8)
SIZES = (2, 4, 1, 1)
STAGES = len(SIZES)


def most_chunks(st):
    most = (RELS * 64 * SIZES[st] + (UNIT - 1) * RELS * TPB) // UNIT
    return -(-most // WIDE[st]) * WIDE[st]


STARTS = tuple(sum(most_chunks(i) for i in range(st)) for st in range(STAGES + 1))
PAY_ROWS = -(-STARTS[-1] * UNIT // (8 * TILE)) * 8
TAB_ROWS = 8
GROUPS = STAGES * RELS * TPB

FLAT = ("chan", "y", "z", "xl", "core")


def flat_index(x, y, z, core):
    return ((((x // 2) * SIDE + y) * SIDE + z) * 2 + x % 2) * 2 + core


def shift(axis_first, axis_second, by):
    pairs = []
    for x in range(SIDE):
        for y in range(SIDE):
            for z in range(SIDE):
                for core in range(2):
                    to = [x, y, z]
                    axis = (axis_first, axis_second)[core]
                    to[axis] = (to[axis] + by) % SIDE
                    pairs.append((flat_index(x, y, z, core), flat_index(*to, core)))
    return pairs


def ring(rows, axis_first, axis_second):
    return [rows] + [lax.ppermute(rows, FLAT, shift(axis_first, axis_second, by)) for by in (1, -1, 2)]


def sibling(rows):
    return lax.ppermute(rows, "core", [(0, 1), (1, 0)])


SMEM = pl.BlockSpec(memory_space=pltpu.SMEM)
VMEM = pl.BlockSpec(memory_space=pltpu.VMEM)
ANY = pl.BlockSpec(memory_space=pl.ANY)


def iota(shape, axis):
    return lax.broadcasted_iota(jnp.int32, shape, axis)


def exact_dot(left, right):
    return jnp.dot(left.astype(jnp.bfloat16), right.astype(jnp.bfloat16), preferred_element_type=jnp.float32)


def sort_kernel(here_ref, packed_ref, pay_ref, tab_ref):
    shape = (SLOTS, BLOCKS)
    my_x, my_y, my_z, my_core = (here_ref[i] for i in range(4))
    block, slot = iota(shape, 1), iota(shape, 0)
    y, z, low, core = block >> 4, (block >> 2) & 3, (block >> 1) & 1, block & 1

    def place(offset):
        offset = offset & 3
        return jnp.where(offset == 0, 0, jnp.where(offset == 3, 1, offset + 1))

    dy, dz = place(y - my_y), place(z - my_z)
    second, third = jnp.where(core == 0, dy, dz), jnp.where(core == 0, dz, dy)
    other = jnp.where(core == my_core, 0, 1)
    stage = jnp.where(third == 0, 0, jnp.where(third == 3, 2 + other, 1))
    buf = jnp.where(third == 0, other, jnp.where(third == 3, 0, (third - 1) * 2 + other))
    lists, at, ids = [], [], []
    for r in range(RELS):
        packed = packed_ref[r]
        cols = (packed >> 2) & 3
        ids.append((packed >> 4) & 31)
        dx = place((cols >> 1) * 2 + low - my_x)
        at.append(buf * 32 + (second * 4 + dx) * 2 + (cols & 1))
        live = slot < (packed >> 9)
        lists.append(jnp.where(live, stage * TPB + (packed & 3), STAGES * TPB))
    members = [
        jnp.where(lists[r] == st * TPB + t, 1.0, 0.0)
        for st in range(STAGES)
        for r in range(RELS)
        for t in range(TPB)
    ]
    member = jnp.concatenate(members, 0)
    lanes = (BLOCKS, BLOCKS)
    ahead = exact_dot(member, jnp.where(iota(lanes, 0) < iota(lanes, 1), 1.0, 0.0))
    row_sum = exact_dot(member, jnp.ones((BLOCKS, TILE), jnp.float32))
    wide = (GROUPS * SLOTS, GROUPS * SLOTS)
    row, col = iota(wide, 0), iota(wide, 1)
    same = (row >> 3) == (col >> 3)
    above = exact_dot(jnp.where(same & (col < row), 1.0, 0.0), row_sum)
    length = exact_dot(jnp.where(same, 1.0, 0.0), row_sum)
    chunks = ((length.astype(jnp.int32) + (UNIT - 1)) >> 2).astype(jnp.float32)
    earlier = ((row >> 7) == (col >> 7)) & ((col >> 3) < (row >> 3)) & ((col & 7) == 0)
    begin = exact_dot(jnp.where(earlier, 1.0, 0.0), chunks)
    step = iota(begin.shape, 0) >> 7
    base = jnp.where(step == 0, STARTS[0], jnp.where(step == 1, STARTS[1], jnp.where(step == 2, STARTS[2], STARTS[3])))
    begin = begin + base.astype(jnp.float32)
    end = (begin + chunks).astype(jnp.int32)
    pos = member * ((begin * UNIT + above)[:, :BLOCKS] + ahead)

    out = jnp.zeros((PAY_ROWS, 2 * TILE), jnp.float32)
    for r in range(RELS):
        where = jnp.zeros(shape, jnp.float32)
        for st in range(STAGES):
            for t in range(TPB):
                first = ((st * RELS + r) * TPB + t) * SLOTS
                where = where + pos[first : first + SLOTS]
        where = jnp.where(lists[r] == STAGES * TPB, -1, where.astype(jnp.int32))
        high, low_part = where >> 7, where & 127
        weight = (ids[r] + (r * POOL - ZERO)).astype(jnp.float32)
        source = at[r].astype(jnp.float32)
        for k in range(SLOTS):
            left = jnp.where(iota((PAY_ROWS, BLOCKS), 0) == high[k : k + 1], 1.0, 0.0)
            hit = iota((TILE, BLOCKS), 0) == low_part[k : k + 1]
            right = jnp.concatenate(
                [jnp.where(hit, weight[k : k + 1], 0.0), jnp.where(hit, source[k : k + 1], 0.0)], 0
            )
            out = out + lax.dot_general(
                left.astype(jnp.bfloat16),
                right.astype(jnp.bfloat16),
                (((1,), (1,)), ((), ())),
                preferred_element_type=jnp.float32,
            )
    out = out.astype(jnp.int32)
    pay_ref[...] = ((out[:, :TILE] + ZERO) << 7) | out[:, TILE:]

    index = iota((TAB_ROWS, TILE), 0) * TILE + iota((TAB_ROWS, TILE), 1)
    table = jnp.zeros((TAB_ROWS, TILE), jnp.int32)
    for st in range(STAGES):
        tile = jnp.zeros((TAB_ROWS, TILE), jnp.int32)
        for g in range(RELS * TPB):
            first = (st * RELS * TPB + g) * SLOTS
            tile = tile + jnp.where(index >= end[first : first + SLOTS], 1, 0)
        inside = (index >= STARTS[st]) & (index < STARTS[st + 1])
        table = jnp.where(inside, jnp.minimum(tile, RELS * TPB - 1), table)
        last = (st * RELS * TPB + RELS * TPB - 1) * SLOTS
        total = end[last : last + SLOTS] - STARTS[st]
        table = jnp.where(index == (TAB_ROWS - 1) * TILE + st, total, table)
    tab_ref[...] = table


def sort_slots(here, packed):
    return pl.pallas_call(
        sort_kernel,
        out_shape=[
            jax.ShapeDtypeStruct((PAY_ROWS, TILE), jnp.int32),
            jax.ShapeDtypeStruct((TAB_ROWS, TILE), jnp.int32),
        ],
        in_specs=[SMEM, VMEM],
        out_specs=[VMEM] * 2,
        compiler_params=pltpu.CompilerParams(vmem_limit_bytes=24 << 20),
        cost_estimate=pl.CostEstimate(flops=0, bytes_accessed=8 << 20, transcendentals=0),
        name="sort_slots",
    )(here, packed)


def stage_kernel(st, count, first, last, *refs):
    refs = list(refs)
    pay, tab = refs[:2]
    del refs[:2]
    if last:
        chan = refs.pop(0)
    pool = refs.pop(0)
    bufs = refs[:count]
    del refs[:count]
    copies = []
    if first:
        total, full, *refs = refs
        copies.append((pool, full.at[pl.ds(0, ZERO)]))
        full[ZERO] = jnp.zeros((TILE, TILE), full.dtype)
        total[...] = jnp.zeros_like(total)
        pool = full
    else:
        before = refs.pop(0)
        if last:
            transforms, selfterm, mine, theirs, total, agg, *refs = refs
            total[...] = before[...]
        else:
            total = refs.pop(0)
    if count > 1:
        rows, sems = refs
        for i, buf in enumerate(bufs):
            size = buf.shape[0]
            copies.append((buf, rows.at[pl.ds(i * size, size)]))
        copies = [pltpu.make_async_copy(*copy, sems.at[i]) for i, copy in enumerate(copies)]
        for copy in copies:
            copy.start()
        for copy in copies:
            copy.wait()
    else:
        rows = bufs[0]

    def turn(i, _):
        for c in range(WIDE[st]):
            chunk = STARTS[st] + i * WIDE[st] + c
            left, right = [], []
            for u in range(UNIT):
                value = pay[chunk >> 5, (chunk & 31) * UNIT + u]
                left.append(pool[value >> 7])
                right.append(rows[value & 127])
            total[tab[chunk >> 7, chunk & 127]] += jnp.dot(
                jnp.concatenate(left, 1), jnp.concatenate(right, 0), preferred_element_type=jnp.float32
            )
        return 0

    turns = (tab[TAB_ROWS - 1, st] + (WIDE[st] - 1)) >> (WIDE[st].bit_length() - 1)
    lax.fori_loop(0, turns, turn, 0)
    if last:
        for t in range(TPB):
            acc = None
            for r in range(RELS):
                part = jnp.dot(
                    total[r * TPB + t].astype(jnp.bfloat16), transforms[r], preferred_element_type=jnp.float32
                )
                acc = part if acc is None else acc + part
            agg[t] = acc
        half = TPB // 2
        for u in range(half):
            mine[u] = agg[chan[0] * half + u] + selfterm[u]
            theirs[u] = agg[(1 - chan[0]) * half + u].astype(jnp.bfloat16)


def run_stage(st, lists, pool, bufs, before=None, tail=None):
    first, last = before is None, tail is not None
    args, specs = list(lists), [SMEM] * 2
    if last:
        args.append(tail[0])
        specs.append(SMEM)
    args += [pool, *bufs]
    specs += [ANY if first else VMEM] + [ANY if len(bufs) > 1 else VMEM] * len(bufs)
    wide = (RELS * TPB, TILE, TILE)
    scratch, aliases = [], {}
    if first:
        out = [
            jax.ShapeDtypeStruct(wide, jnp.float32),
            jax.ShapeDtypeStruct((ZERO + 1, TILE, TILE), pool.dtype),
        ]
    else:
        args.append(before)
        specs.append(VMEM)
        if last:
            args += tail[1:]
            specs += [VMEM] * 2
            half = (TPB // 2, TILE, TILE)
            out = [jax.ShapeDtypeStruct(half, jnp.float32), jax.ShapeDtypeStruct(half, jnp.bfloat16)]
            scratch = [pltpu.VMEM(wide, jnp.float32), pltpu.VMEM((TPB, TILE, TILE), jnp.float32)]
        else:
            out = [jax.ShapeDtypeStruct(wide, jnp.float32)]
            aliases = {len(args) - 1: 0}
    if len(bufs) > 1:
        scratch.append(pltpu.VMEM((32 * SIZES[st], TILE, TILE), jnp.bfloat16))
        scratch.append(pltpu.SemaphoreType.DMA((len(bufs) + 1,)))
    slots = 16 * 8 * SIZES[st]
    return pl.pallas_call(
        functools.partial(stage_kernel, st, len(bufs), first, last),
        out_shape=out,
        in_specs=specs,
        out_specs=[VMEM] * len(out),
        scratch_shapes=scratch,
        input_output_aliases=aliases,
        compiler_params=pltpu.CompilerParams(vmem_limit_bytes=24 << 20),
        cost_estimate=pl.CostEstimate(
            flops=slots * 2 * TILE**3 * 4, bytes_accessed=(6 + SIZES[st]) << 20, transcendentals=0
        ),
        name=f"stage{st}",
    )(*args)


def shards(features, transforms, self_weight, tile_rows, tile_cols, tile_ids, tile_count, tile_pool):
    chan, xl = lax.axis_index("chan"), lax.axis_index("xl")
    own = features[0, 0]
    half_rows, width = own.shape
    here = jnp.stack(
        [chan * 2 + xl, lax.axis_index("y"), lax.axis_index("z"), lax.axis_index("core")]
    ).astype(jnp.int32)

    def by_slot(table):
        return table[:, 0].transpose(0, 2, 1)

    line = jnp.concatenate(ring(own, 0, 0), 0)
    selfterm = jnp.dot(own, self_weight, preferred_element_type=jnp.float32).reshape(-1, TILE, width)
    now = lax.dynamic_slice_in_dim(transforms, chan * RELS, RELS, 0)
    packed = by_slot(tile_rows) | (by_slot(tile_cols) << 2) | (by_slot(tile_ids) << 4)
    packed = packed | (tile_count[:, 0][:, None, :] << 9)
    line, packed, selfterm, now = lax.optimization_barrier((line, packed, selfterm, now))
    plane = jnp.concatenate(ring(line, 1, 2), 0)
    lists = sort_slots(here, packed)
    plane, lists = lax.optimization_barrier((plane, lists))
    plane = plane.reshape(-1, TILE, width)
    left = lax.ppermute(plane, FLAT, shift(2, 1, 1))
    right = lax.ppermute(plane, FLAT, shift(2, 1, -1))
    pool = tile_pool.reshape(RELS * POOL, TILE, TILE)
    total, pool = run_stage(0, lists, pool, [plane, sibling(plane)])
    left, right, total = lax.optimization_barrier((left, right, total))
    half = plane.shape[0] // 2
    far = [
        lax.ppermute(left[:half], FLAT, shift(2, 1, 1)),
        lax.ppermute(right[half:], FLAT, shift(2, 1, -1)),
    ]
    total = run_stage(1, lists, pool, [left, sibling(left), right, sibling(right)], total)[0]
    *far, total = lax.optimization_barrier((*far, total))
    beyond = [sibling(piece) for piece in far]
    total = run_stage(2, lists, pool, far, total)[0]
    kept, sent = run_stage(3, lists, pool, beyond, total, (here[:1] >> 1, now, selfterm))
    got = lax.ppermute(sent, "chan", [(0, 1), (1, 0)])
    updated = jax.nn.relu(kept + got.astype(jnp.float32)).astype(jnp.bfloat16)
    return updated.reshape(1, 1, half_rows, width)


def solution(mesh):
    fine = Mesh(mesh.devices.reshape(2, SIDE, SIDE, 2, 2), FLAT)
    blk = ("y", "z", "xl", "core")
    placed = (
        P(blk, "chan", None, None),
        P(),
        P(),
        P("chan", blk, None, None),
        P("chan", blk, None, None),
        P("chan", blk, None, None),
        P("chan", blk, None),
        P("chan", blk, None, None, None),
    )
    return jax.shard_map(
        shards, mesh=fine, in_specs=placed, out_specs=P(blk, "chan", None, None), check_vma=False
    )
```

```python
import functools

import jax
import jax.numpy as jnp
from jax import lax
from jax.experimental import pallas as pl
from jax.experimental.pallas import tpu as pltpu
from jax.sharding import Mesh, PartitionSpec as P

SIDE = 4
TILE = 128
RELS = 4
POOL = 32
TPB = 4
SLOTS = 8
BLOCKS = 64
ZERO = RELS * POOL
UNIT = 4
WIDE = (16, 16, 8, 8, 8)
SIZES = (64, 128, 16, 32, 16)
STAGES = len(SIZES)
FLOPS = (4 << 30, 8 << 30, 1 << 30, 2 << 30, 1 << 30)


def most_chunks(st):
    most = (RELS * 2 * SIZES[st] + (UNIT - 1) * RELS * TPB) // UNIT
    return -(-most // WIDE[st]) * WIDE[st]


STARTS = tuple(sum(most_chunks(i) for i in range(st)) for st in range(STAGES + 1))
PAY_ROWS = -(-STARTS[-1] * UNIT // (8 * TILE)) * 8
TAB_ROWS = 8
GROUPS = STAGES * RELS * TPB

FLAT = ("chan", "y", "z", "xl", "core")


def flat_index(x, y, z, core):
    return ((((x // 2) * SIDE + y) * SIDE + z) * 2 + x % 2) * 2 + core


def shift(axis_first, axis_second, by):
    pairs = []
    for x in range(SIDE):
        for y in range(SIDE):
            for z in range(SIDE):
                for core in range(2):
                    to = [x, y, z]
                    axis = (axis_first, axis_second)[core]
                    to[axis] = (to[axis] + by) % SIDE
                    pairs.append((flat_index(x, y, z, core), flat_index(*to, core)))
    return pairs


def ring(rows, axis_first, axis_second):
    return [rows] + [lax.ppermute(rows, FLAT, shift(axis_first, axis_second, by)) for by in (1, -1, 2)]


def sibling(rows):
    return lax.ppermute(rows, "core", [(0, 1), (1, 0)])


SMEM = pl.BlockSpec(memory_space=pltpu.SMEM)
VMEM = pl.BlockSpec(memory_space=pltpu.VMEM)
ANY = pl.BlockSpec(memory_space=pl.ANY)


def iota(shape, axis):
    return lax.broadcasted_iota(jnp.int32, shape, axis)


def exact_dot(left, right):
    return jnp.dot(left.astype(jnp.bfloat16), right.astype(jnp.bfloat16), preferred_element_type=jnp.float32)


def sort_kernel(here_ref, packed_ref, pool_hbm, pay_ref, tab_ref, pool_ref, sem):
    fetch = pltpu.make_async_copy(pool_hbm, pool_ref.at[pl.ds(0, ZERO)], sem)
    fetch.start()
    pool_ref[ZERO] = jnp.zeros((TILE, TILE), pool_ref.dtype)
    shape = (SLOTS, BLOCKS)
    my_x, my_y, my_z, my_core = (here_ref[i] for i in range(4))
    block, slot = iota(shape, 1), iota(shape, 0)
    y, z, low, core = block >> 4, (block >> 2) & 3, (block >> 1) & 1, block & 1

    def place(offset):
        offset = offset & 3
        return jnp.where(offset == 0, 0, jnp.where(offset == 3, 1, offset + 1))

    dy, dz = place(y - my_y), place(z - my_z)
    second, third = jnp.where(core == 0, dy, dz), jnp.where(core == 0, dz, dy)
    other = jnp.where(core == my_core, 0, 1)
    far_stage = jnp.where(second < 2, 2, 3) + other
    stage = jnp.where(third == 3, far_stage, jnp.where(third == 0, 0, 1))
    buf = jnp.where(third == 3, jnp.where(far_stage == 4, -16, 0), (jnp.where(third == 2, 2, 0) + other) * 32)
    lists, at, ids = [], [], []
    for r in range(RELS):
        packed = packed_ref[r]
        cols = (packed >> 2) & 3
        ids.append((packed >> 4) & 31)
        dx = place((cols >> 1) * 2 + low - my_x)
        at.append(buf + (second * 4 + dx) * 2 + (cols & 1))
        live = slot < (packed >> 9)
        lists.append(jnp.where(live, stage * TPB + (packed & 3), STAGES * TPB))
    members = [
        jnp.where(lists[r] == st * TPB + t, 1.0, 0.0)
        for st in range(STAGES)
        for r in range(RELS)
        for t in range(TPB)
    ]
    member = jnp.concatenate(members, 0)
    lanes = (BLOCKS, BLOCKS)
    ahead = exact_dot(member, jnp.where(iota(lanes, 0) < iota(lanes, 1), 1.0, 0.0))
    row_sum = exact_dot(member, jnp.ones((BLOCKS, TILE), jnp.float32))
    wide = (GROUPS * SLOTS, GROUPS * SLOTS)
    row, col = iota(wide, 0), iota(wide, 1)
    same = (row >> 3) == (col >> 3)
    above = exact_dot(jnp.where(same & (col < row), 1.0, 0.0), row_sum)
    length = exact_dot(jnp.where(same, 1.0, 0.0), row_sum)
    chunks = ((length.astype(jnp.int32) + (UNIT - 1)) >> 2).astype(jnp.float32)
    earlier = ((row >> 7) == (col >> 7)) & ((col >> 3) < (row >> 3)) & ((col & 7) == 0)
    begin = exact_dot(jnp.where(earlier, 1.0, 0.0), chunks)
    step = iota(begin.shape, 0) >> 7
    base = jnp.zeros_like(step)
    for st in range(1, STAGES):
        base = jnp.where(step == st, STARTS[st], base)
    begin = begin + base.astype(jnp.float32)
    end = (begin + chunks).astype(jnp.int32)
    pos = member * ((begin * UNIT + above)[:, :BLOCKS] + ahead)

    out = jnp.zeros((PAY_ROWS, 2 * TILE), jnp.float32)
    for r in range(RELS):
        where = jnp.zeros(shape, jnp.float32)
        for st in range(STAGES):
            for t in range(TPB):
                first = ((st * RELS + r) * TPB + t) * SLOTS
                where = where + pos[first : first + SLOTS]
        where = jnp.where(lists[r] == STAGES * TPB, -1, where.astype(jnp.int32))
        high, low_part = where >> 7, where & 127
        weight = (ids[r] + (r * POOL - ZERO)).astype(jnp.float32)
        source = at[r].astype(jnp.float32)
        for k in range(SLOTS):
            left = jnp.where(iota((PAY_ROWS, BLOCKS), 0) == high[k : k + 1], 1.0, 0.0)
            hit = iota((TILE, BLOCKS), 0) == low_part[k : k + 1]
            right = jnp.concatenate(
                [jnp.where(hit, weight[k : k + 1], 0.0), jnp.where(hit, source[k : k + 1], 0.0)], 0
            )
            out = out + lax.dot_general(
                left.astype(jnp.bfloat16),
                right.astype(jnp.bfloat16),
                (((1,), (1,)), ((), ())),
                preferred_element_type=jnp.float32,
            )
    out = out.astype(jnp.int32)
    pay_ref[...] = ((out[:, :TILE] + ZERO) << 7) | out[:, TILE:]

    index = iota((TAB_ROWS, TILE), 0) * TILE + iota((TAB_ROWS, TILE), 1)
    table = jnp.zeros((TAB_ROWS, TILE), jnp.int32)
    for st in range(STAGES):
        tile = jnp.zeros((TAB_ROWS, TILE), jnp.int32)
        for g in range(RELS * TPB):
            first = (st * RELS * TPB + g) * SLOTS
            tile = tile + jnp.where(index >= end[first : first + SLOTS], 1, 0)
        inside = (index >= STARTS[st]) & (index < STARTS[st + 1])
        table = jnp.where(inside, jnp.minimum(tile, RELS * TPB - 1), table)
        last = (st * RELS * TPB + RELS * TPB - 1) * SLOTS
        total = end[last : last + SLOTS] - STARTS[st]
        table = jnp.where(index == (TAB_ROWS - 1) * TILE + st, total, table)
    tab_ref[...] = table
    fetch.wait()


def sort_slots(here, packed, pool):
    return pl.pallas_call(
        sort_kernel,
        out_shape=[
            jax.ShapeDtypeStruct((PAY_ROWS, TILE), jnp.int32),
            jax.ShapeDtypeStruct((TAB_ROWS, TILE), jnp.int32),
            jax.ShapeDtypeStruct((ZERO + 1, TILE, TILE), pool.dtype),
        ],
        in_specs=[SMEM, VMEM, ANY],
        out_specs=[VMEM] * 3,
        scratch_shapes=[pltpu.SemaphoreType.DMA],
        compiler_params=pltpu.CompilerParams(vmem_limit_bytes=24 << 20),
        cost_estimate=pl.CostEstimate(flops=0, bytes_accessed=8 << 20, transcendentals=0),
        name="sort_slots",
    )(here, packed, pool)


def stage_kernel(st, count, first, last, *refs):
    refs = list(refs)
    pay, tab = refs[:2]
    del refs[:2]
    if last:
        chan = refs.pop(0)
    pool = refs.pop(0)
    bufs = refs[:count]
    del refs[:count]
    copies = []
    if first:
        total = refs.pop(0)
        total[...] = jnp.zeros_like(total)
    else:
        before = refs.pop(0)
        if last:
            transforms, selfterm, mine, theirs, total, agg, *refs = refs
            total[...] = before[...]
        else:
            total = refs.pop(0)
    if count > 1:
        rows, sems = refs
        at = 0
        for buf in bufs:
            copies.append((buf, rows.at[pl.ds(at, buf.shape[0])]))
            at += buf.shape[0]
        copies = [pltpu.make_async_copy(*copy, sems.at[i]) for i, copy in enumerate(copies)]
        for copy in copies:
            copy.start()
        for copy in copies:
            copy.wait()
    else:
        rows = bufs[0]

    def turn(i, _):
        for c in range(WIDE[st]):
            chunk = STARTS[st] + i * WIDE[st] + c
            left, right = [], []
            for u in range(UNIT):
                value = pay[chunk >> 5, (chunk & 31) * UNIT + u]
                left.append(pool[value >> 7])
                right.append(rows[value & 127])
            total[tab[chunk >> 7, chunk & 127]] += jnp.dot(
                jnp.concatenate(left, 1), jnp.concatenate(right, 0), preferred_element_type=jnp.float32
            )
        return 0

    turns = (tab[TAB_ROWS - 1, st] + (WIDE[st] - 1)) >> (WIDE[st].bit_length() - 1)
    lax.fori_loop(0, turns, turn, 0)
    if last:
        for t in range(TPB):
            acc = None
            for r in range(RELS):
                part = jnp.dot(
                    total[r * TPB + t].astype(jnp.bfloat16), transforms[r], preferred_element_type=jnp.float32
                )
                acc = part if acc is None else acc + part
            agg[t] = acc
        half = TPB // 2
        for u in range(half):
            mine[u] = agg[chan[0] * half + u] + selfterm[u]
            theirs[u] = agg[(1 - chan[0]) * half + u].astype(jnp.bfloat16)


def run_stage(st, lists, pool, bufs, before=None, tail=None):
    first, last = before is None, tail is not None
    args, specs = list(lists), [SMEM] * 2
    if last:
        args.append(tail[0])
        specs.append(SMEM)
    args += [pool, *bufs]
    specs += [VMEM] + [ANY if len(bufs) > 1 else VMEM] * len(bufs)
    wide = (RELS * TPB, TILE, TILE)
    scratch, aliases = [], {}
    if first:
        out = [jax.ShapeDtypeStruct(wide, jnp.float32)]
    else:
        args.append(before)
        specs.append(VMEM)
        if last:
            args += tail[1:]
            specs += [VMEM] * 2
            half = (TPB // 2, TILE, TILE)
            out = [jax.ShapeDtypeStruct(half, jnp.float32), jax.ShapeDtypeStruct(half, jnp.bfloat16)]
            scratch = [pltpu.VMEM(wide, jnp.float32), pltpu.VMEM((TPB, TILE, TILE), jnp.float32)]
        else:
            out = [jax.ShapeDtypeStruct(wide, jnp.float32)]
            aliases = {len(args) - 1: 0}
    if len(bufs) > 1:
        scratch.append(pltpu.VMEM((SIZES[st], TILE, TILE), jnp.bfloat16))
        scratch.append(pltpu.SemaphoreType.DMA((len(bufs),)))
    return pl.pallas_call(
        functools.partial(stage_kernel, st, len(bufs), first, last),
        out_shape=out,
        in_specs=specs,
        out_specs=[VMEM] * len(out),
        scratch_shapes=scratch,
        input_output_aliases=aliases,
        compiler_params=pltpu.CompilerParams(vmem_limit_bytes=24 << 20),
        cost_estimate=pl.CostEstimate(flops=FLOPS[st], bytes_accessed=8 << 20, transcendentals=0),
        name=f"stage{st}",
    )(*args)


def shards(features, transforms, self_weight, tile_rows, tile_cols, tile_ids, tile_count, tile_pool):
    chan, xl = lax.axis_index("chan"), lax.axis_index("xl")
    own = features[0, 0]
    half_rows, width = own.shape
    here = jnp.stack(
        [chan * 2 + xl, lax.axis_index("y"), lax.axis_index("z"), lax.axis_index("core")]
    ).astype(jnp.int32)

    def by_slot(table):
        return table[:, 0].transpose(0, 2, 1)

    line = jnp.concatenate(ring(own, 0, 0), 0)
    selfterm = jnp.dot(own, self_weight, preferred_element_type=jnp.float32).reshape(-1, TILE, width)
    now = lax.dynamic_slice_in_dim(transforms, chan * RELS, RELS, 0)
    packed = by_slot(tile_rows) | (by_slot(tile_cols) << 2) | (by_slot(tile_ids) << 4)
    packed = packed | (tile_count[:, 0][:, None, :] << 9)
    line, packed, selfterm, now = lax.optimization_barrier((line, packed, selfterm, now))
    plane = jnp.concatenate(ring(line, 1, 2), 0)
    pool = tile_pool.reshape(RELS * POOL, TILE, TILE)
    pay, tab, pool = sort_slots(here, packed, pool)
    lists = (pay, tab)
    plane, lists, pool = lax.optimization_barrier((plane, lists, pool))
    plane = plane.reshape(-1, TILE, width)
    left = lax.ppermute(plane, FLAT, shift(2, 1, 1))
    right = lax.ppermute(plane, FLAT, shift(2, 1, -1))
    total = run_stage(0, lists, pool, [plane, sibling(plane)])[0]
    left, right, total = lax.optimization_barrier((left, right, total))
    half = plane.shape[0] // 2
    first = lax.ppermute(left[:half], FLAT, shift(2, 1, 1))
    second = lax.ppermute(right[half:], FLAT, shift(2, 1, -1))
    total = run_stage(1, lists, pool, [left, sibling(left), right, sibling(right)], total)[0]
    first, total = lax.optimization_barrier((first, total))
    other = sibling(first)
    total = run_stage(2, lists, pool, [first], total)[0]
    second, total = lax.optimization_barrier((second, total))
    last = sibling(second)
    total = run_stage(3, lists, pool, [other, second], total)[0]
    kept, sent = run_stage(4, lists, pool, [last], total, (here[:1] >> 1, now, selfterm))
    got = lax.ppermute(sent, "chan", [(0, 1), (1, 0)])
    updated = jax.nn.relu(kept + got.astype(jnp.float32)).astype(jnp.bfloat16)
    return updated.reshape(1, 1, half_rows, width)


def solution(mesh):
    fine = Mesh(mesh.devices.reshape(2, SIDE, SIDE, 2, 2), FLAT)
    blk = ("y", "z", "xl", "core")
    placed = (
        P(blk, "chan", None, None),
        P(),
        P(),
        P("chan", blk, None, None),
        P("chan", blk, None, None),
        P("chan", blk, None, None),
        P("chan", blk, None),
        P("chan", blk, None, None, None),
    )
    return jax.shard_map(
        shards, mesh=fine, in_specs=placed, out_specs=P(blk, "chan", None, None), check_vma=False
    )
```

```python
import functools

import jax
import jax.numpy as jnp
from jax import lax
from jax.experimental import pallas as pl
from jax.experimental.pallas import tpu as pltpu
from jax.sharding import Mesh, PartitionSpec as P

SIDE = 4
TILE = 128
RELS = 4
POOL = 32
TPB = 4
SLOTS = 8
BLOCKS = 64
ZERO = RELS * POOL
UNIT = 4
WIDE = (16, 16, 8, 8, 8, 8)
SIZES = (64, 128, 16, 32, 16, 64)
STAGES = len(SIZES)
FLOPS = (4 << 30, 8 << 30, 1 << 30, 2 << 30, 1 << 30, 2 << 30)


def most_chunks(st):
    most = (RELS * 2 * SIZES[st] + (UNIT - 1) * RELS * TPB) // UNIT
    return -(-most // WIDE[st]) * WIDE[st]


STARTS = tuple(sum(most_chunks(i) for i in range(st)) for st in range(STAGES + 1))
PAY_ROWS = -(-STARTS[-1] * UNIT // (8 * TILE)) * 8
TAB_ROWS = 8
GROUPS = STAGES * RELS * TPB

FLAT = ("chan", "y", "z", "xl", "core")


def flat_index(x, y, z, core):
    return ((((x // 2) * SIDE + y) * SIDE + z) * 2 + x % 2) * 2 + core


def shift(axis_first, axis_second, by):
    pairs = []
    for x in range(SIDE):
        for y in range(SIDE):
            for z in range(SIDE):
                for core in range(2):
                    to = [x, y, z]
                    axis = (axis_first, axis_second)[core]
                    to[axis] = (to[axis] + by) % SIDE
                    pairs.append((flat_index(x, y, z, core), flat_index(*to, core)))
    return pairs


def ring(rows, axis_first, axis_second):
    return [rows] + [lax.ppermute(rows, FLAT, shift(axis_first, axis_second, by)) for by in (1, -1, 2)]


def sibling(rows):
    return lax.ppermute(rows, "core", [(0, 1), (1, 0)])


SMEM = pl.BlockSpec(memory_space=pltpu.SMEM)
VMEM = pl.BlockSpec(memory_space=pltpu.VMEM)
ANY = pl.BlockSpec(memory_space=pl.ANY)


def iota(shape, axis):
    return lax.broadcasted_iota(jnp.int32, shape, axis)


def exact_dot(left, right):
    return jnp.dot(left.astype(jnp.bfloat16), right.astype(jnp.bfloat16), preferred_element_type=jnp.float32)


def sort_kernel(here_ref, packed_ref, pool_hbm, pay_ref, tab_ref, pool_ref, sem):
    fetch = pltpu.make_async_copy(pool_hbm, pool_ref.at[pl.ds(0, ZERO)], sem)
    fetch.start()
    pool_ref[ZERO] = jnp.zeros((TILE, TILE), pool_ref.dtype)
    shape = (SLOTS, BLOCKS)
    my_x, my_y, my_z, my_core = (here_ref[i] for i in range(4))
    block, slot = iota(shape, 1), iota(shape, 0)
    y, z, low, core = block >> 4, (block >> 2) & 3, (block >> 1) & 1, block & 1

    def place(offset):
        offset = offset & 3
        return jnp.where(offset == 0, 0, jnp.where(offset == 3, 1, offset + 1))

    dy, dz = place(y - my_y), place(z - my_z)
    second, third = jnp.where(core == 0, dy, dz), jnp.where(core == 0, dz, dy)
    other = jnp.where(core == my_core, 0, 1)
    far_stage = jnp.where(second < 2, 2, 3) + other
    stage = jnp.where(third == 3, far_stage, jnp.where(third == 0, 0, 1))
    buf = jnp.where(third == 3, jnp.where(far_stage == 4, -16, 0), (jnp.where(third == 2, 2, 0) + other) * 32)
    lists, at, ids = [], [], []
    for r in range(RELS):
        packed = packed_ref[r]
        tile, cols = packed & 3, (packed >> 2) & 3
        ids.append((packed >> 4) & 31)
        stays = (third == 3) & ((tile >> 1) == (my_x >> 1))
        dx = place((cols >> 1) * 2 + low - my_x)
        at.append(jnp.where(stays, other * 32, buf) + (second * 4 + dx) * 2 + (cols & 1))
        live = slot < (packed >> 9)
        lists.append(jnp.where(live, jnp.where(stays, STAGES - 1, stage) * TPB + tile, STAGES * TPB))
    square = (RELS * TPB * SLOTS, RELS * TPB * SLOTS)
    row, col = iota(square, 0), iota(square, 1)
    same = (row >> 3) == (col >> 3)
    before = jnp.where(same & (col < row), 1.0, 0.0)
    whole = jnp.where(same, 1.0, 0.0)
    earlier = jnp.where(((col >> 3) < (row >> 3)) & ((col & 7) == 0), 1.0, 0.0)
    lanes = (BLOCKS, BLOCKS)
    upper = jnp.where(iota(lanes, 0) < iota(lanes, 1), 1.0, 0.0)
    ones = jnp.ones((BLOCKS, TILE), jnp.float32)
    pos, end = [], []
    for st in range(STAGES):
        member = jnp.concatenate(
            [jnp.where(lists[r] == st * TPB + t, 1.0, 0.0) for r in range(RELS) for t in range(TPB)], 0
        )
        row_sum = exact_dot(member, ones)
        above = exact_dot(before, row_sum)
        length = exact_dot(whole, row_sum)
        chunks = ((length.astype(jnp.int32) + (UNIT - 1)) >> 2).astype(jnp.float32)
        begin = exact_dot(earlier, chunks) + STARTS[st]
        end.append((begin + chunks).astype(jnp.int32))
        pos.append(member * ((begin * UNIT + above)[:, :BLOCKS] + exact_dot(member, upper)))

    out = jnp.zeros((PAY_ROWS, 2 * TILE), jnp.float32)
    for r in range(RELS):
        where = jnp.zeros(shape, jnp.float32)
        for st in range(STAGES):
            for t in range(TPB):
                first = (r * TPB + t) * SLOTS
                where = where + pos[st][first : first + SLOTS]
        where = jnp.where(lists[r] == STAGES * TPB, -1, where.astype(jnp.int32))
        high, low_part = where >> 7, where & 127
        weight = (ids[r] + (r * POOL - ZERO)).astype(jnp.float32)
        source = at[r].astype(jnp.float32)
        for k in range(SLOTS):
            left = jnp.where(iota((PAY_ROWS, BLOCKS), 0) == high[k : k + 1], 1.0, 0.0)
            hit = iota((TILE, BLOCKS), 0) == low_part[k : k + 1]
            right = jnp.concatenate(
                [jnp.where(hit, weight[k : k + 1], 0.0), jnp.where(hit, source[k : k + 1], 0.0)], 0
            )
            out = out + lax.dot_general(
                left.astype(jnp.bfloat16),
                right.astype(jnp.bfloat16),
                (((1,), (1,)), ((), ())),
                preferred_element_type=jnp.float32,
            )
    out = out.astype(jnp.int32)
    pay_ref[...] = ((out[:, :TILE] + ZERO) << 7) | out[:, TILE:]

    index = iota((TAB_ROWS, TILE), 0) * TILE + iota((TAB_ROWS, TILE), 1)
    table = jnp.zeros((TAB_ROWS, TILE), jnp.int32)
    for st in range(STAGES):
        tile = jnp.zeros((TAB_ROWS, TILE), jnp.int32)
        for g in range(RELS * TPB):
            tile = tile + jnp.where(index >= end[st][g * SLOTS : (g + 1) * SLOTS], 1, 0)
        inside = (index >= STARTS[st]) & (index < STARTS[st + 1])
        table = jnp.where(inside, jnp.minimum(tile, RELS * TPB - 1), table)
        total = end[st][-SLOTS:] - STARTS[st]
        table = jnp.where(index == (TAB_ROWS - 1) * TILE + st, total, table)
    tab_ref[...] = table
    fetch.wait()


def sort_slots(here, packed, pool):
    return pl.pallas_call(
        sort_kernel,
        out_shape=[
            jax.ShapeDtypeStruct((PAY_ROWS, TILE), jnp.int32),
            jax.ShapeDtypeStruct((TAB_ROWS, TILE), jnp.int32),
            jax.ShapeDtypeStruct((ZERO + 1, TILE, TILE), pool.dtype),
        ],
        in_specs=[SMEM, VMEM, ANY],
        out_specs=[VMEM] * 3,
        scratch_shapes=[pltpu.SemaphoreType.DMA],
        compiler_params=pltpu.CompilerParams(vmem_limit_bytes=24 << 20),
        cost_estimate=pl.CostEstimate(flops=0, bytes_accessed=8 << 20, transcendentals=0),
        name="sort_slots",
    )(here, packed, pool)


def stage_kernel(st, count, *refs):
    refs = list(refs)
    pay, tab, pool = refs[:3]
    bufs = refs[3 : 3 + count]
    del refs[: 3 + count]
    copies = []
    if st == 0:
        total = refs.pop(0)
        total[...] = jnp.zeros_like(total)
    elif st < STAGES - 2:
        _, total, *refs = refs
    elif st == STAGES - 2:
        _, chan, transforms, total, theirs, *refs = refs
    else:
        before, chan, transforms, selfterm, mine, total, *refs = refs
        total[...] = before[...]
    if count > 1:
        rows, sems = refs
        at = 0
        for buf in bufs:
            copies.append((buf, rows.at[pl.ds(at, buf.shape[0])]))
            at += buf.shape[0]
        copies = [pltpu.make_async_copy(*copy, sems.at[i]) for i, copy in enumerate(copies)]
        for copy in copies:
            copy.start()
        for copy in copies:
            copy.wait()
    else:
        rows = bufs[0]

    def turn(i, _):
        for c in range(WIDE[st]):
            chunk = STARTS[st] + i * WIDE[st] + c
            left, right = [], []
            for u in range(UNIT):
                value = pay[chunk >> 5, (chunk & 31) * UNIT + u]
                left.append(pool[value >> 7])
                right.append(rows[value & 127])
            total[tab[chunk >> 7, chunk & 127]] += jnp.dot(
                jnp.concatenate(left, 1), jnp.concatenate(right, 0), preferred_element_type=jnp.float32
            )
        return 0

    turns = (tab[TAB_ROWS - 1, st] + (WIDE[st] - 1)) >> (WIDE[st].bit_length() - 1)
    lax.fori_loop(0, turns, turn, 0)

    def final(tile):
        parts = [
            jnp.dot(total[r * TPB + tile].astype(jnp.bfloat16), transforms[r], preferred_element_type=jnp.float32)
            for r in range(RELS)
        ]
        return (parts[0] + parts[1]) + (parts[2] + parts[3])

    half = TPB // 2
    for u in range(half):
        if st == STAGES - 2:
            theirs[u] = final((1 - chan[0]) * half + u).astype(jnp.bfloat16)
        if st == STAGES - 1:
            mine[u] = final(chan[0] * half + u) + selfterm[u]


def run_stage(st, lists, pool, bufs, *more):
    args = [*lists, pool, *bufs, *more]
    specs = [SMEM] * 2 + [VMEM] + [ANY if len(bufs) > 1 else VMEM] * len(bufs)
    specs += [VMEM, SMEM, VMEM, VMEM][: len(more)]
    wide = (RELS * TPB, TILE, TILE)
    half = (TPB // 2, TILE, TILE)
    out = [jax.ShapeDtypeStruct(wide, jnp.float32)]
    scratch, aliases = [], {}
    if st == STAGES - 1:
        out = [jax.ShapeDtypeStruct(half, jnp.float32)]
        scratch = [pltpu.VMEM(wide, jnp.float32)]
    elif st > 0:
        aliases = {3 + len(bufs): 0}
    if st == STAGES - 2:
        out.append(jax.ShapeDtypeStruct(half, jnp.bfloat16))
    if len(bufs) > 1:
        scratch.append(pltpu.VMEM((SIZES[st], TILE, TILE), jnp.bfloat16))
        scratch.append(pltpu.SemaphoreType.DMA((len(bufs),)))
    return pl.pallas_call(
        functools.partial(stage_kernel, st, len(bufs)),
        out_shape=out,
        in_specs=specs,
        out_specs=[VMEM] * len(out),
        scratch_shapes=scratch,
        input_output_aliases=aliases,
        compiler_params=pltpu.CompilerParams(vmem_limit_bytes=24 << 20),
        cost_estimate=pl.CostEstimate(flops=FLOPS[st], bytes_accessed=8 << 20, transcendentals=0),
        name=f"stage{st}",
    )(*args)


def shards(features, transforms, self_weight, tile_rows, tile_cols, tile_ids, tile_count, tile_pool):
    chan, xl = lax.axis_index("chan"), lax.axis_index("xl")
    own = features[0, 0]
    half_rows, width = own.shape
    here = jnp.stack(
        [chan * 2 + xl, lax.axis_index("y"), lax.axis_index("z"), lax.axis_index("core")]
    ).astype(jnp.int32)

    def by_slot(table):
        return table[:, 0].transpose(0, 2, 1)

    line = jnp.concatenate(ring(own, 0, 0), 0)
    selfterm = jnp.dot(own, self_weight, preferred_element_type=jnp.float32).reshape(-1, TILE, width)
    now = lax.dynamic_slice_in_dim(transforms, chan * RELS, RELS, 0)
    packed = by_slot(tile_rows) | (by_slot(tile_cols) << 2) | (by_slot(tile_ids) << 4)
    packed = packed | (tile_count[:, 0][:, None, :] << 9)
    line, packed, selfterm, now = lax.optimization_barrier((line, packed, selfterm, now))
    plane = jnp.concatenate(ring(line, 1, 2), 0)
    pool = tile_pool.reshape(RELS * POOL, TILE, TILE)
    pay, tab, pool = sort_slots(here, packed, pool)
    lists = (pay, tab)
    plane, lists, pool = lax.optimization_barrier((plane, lists, pool))
    plane = plane.reshape(-1, TILE, width)
    left = lax.ppermute(plane, FLAT, shift(2, 1, 1))
    right = lax.ppermute(plane, FLAT, shift(2, 1, -1))
    total = run_stage(0, lists, pool, [plane, sibling(plane)])[0]
    left, right, total = lax.optimization_barrier((left, right, total))
    half = plane.shape[0] // 2
    first = lax.ppermute(left[:half], FLAT, shift(2, 1, 1))
    second = lax.ppermute(right[half:], FLAT, shift(2, 1, -1))
    total = run_stage(1, lists, pool, [left, sibling(left), right, sibling(right)], total)[0]
    first, total = lax.optimization_barrier((first, total))
    other = sibling(first)
    total = run_stage(2, lists, pool, [first], total)[0]
    second, total = lax.optimization_barrier((second, total))
    last = sibling(second)
    total = run_stage(3, lists, pool, [other, second], total)[0]
    total, sent = run_stage(4, lists, pool, [last], total, here[:1] >> 1, now)
    got = lax.ppermute(sent, "chan", [(0, 1), (1, 0)])
    kept = run_stage(5, lists, pool, [first, second, other, last], total, here[:1] >> 1, now, selfterm)[0]
    updated = jax.nn.relu(kept + got.astype(jnp.float32)).astype(jnp.bfloat16)
    return updated.reshape(1, 1, half_rows, width)


def solution(mesh):
    fine = Mesh(mesh.devices.reshape(2, SIDE, SIDE, 2, 2), FLAT)
    blk = ("y", "z", "xl", "core")
    placed = (
        P(blk, "chan", None, None),
        P(),
        P(),
        P("chan", blk, None, None),
        P("chan", blk, None, None),
        P("chan", blk, None, None),
        P("chan", blk, None),
        P("chan", blk, None, None, None),
    )
    return jax.shard_map(
        shards, mesh=fine, in_specs=placed, out_specs=P(blk, "chan", None, None), check_vma=False
    )
```

```python
import functools

import jax
import jax.numpy as jnp
from jax import lax
from jax.experimental import pallas as pl
from jax.experimental.pallas import tpu as pltpu
from jax.sharding import Mesh, PartitionSpec as P

SIDE = 4
TILE = 128
RELS = 4
POOL = 32
TPB = 4
SLOTS = 8
BLOCKS = 64
ZERO = RELS * POOL
UNIT = 4
WIDE = (16, 16, 8, 8, 8, 8)
SIZES = (64, 128, 16, 32, 16, 64)
STAGES = len(SIZES)
FLOPS = (4 << 30, 8 << 30, 1 << 30, 2 << 30, 1 << 30, 2 << 30)


def most_chunks(st):
    most = (RELS * 2 * SIZES[st] + (UNIT - 1) * RELS * TPB) // UNIT
    return -(-most // WIDE[st]) * WIDE[st]


STARTS = tuple(sum(most_chunks(i) for i in range(st)) for st in range(STAGES + 1))
PAY_ROWS = -(-STARTS[-1] * UNIT // (8 * TILE)) * 8
PAY_SPANS = tuple((STARTS[st] * UNIT // TILE, -(-STARTS[st + 1] * UNIT // TILE)) for st in range(STAGES))
TAB_ROWS = 8
GROUPS = STAGES * RELS * TPB

FLAT = ("chan", "y", "z", "xl", "core")


def flat_index(x, y, z, core):
    return ((((x // 2) * SIDE + y) * SIDE + z) * 2 + x % 2) * 2 + core


def shift(axis_first, axis_second, by):
    pairs = []
    for x in range(SIDE):
        for y in range(SIDE):
            for z in range(SIDE):
                for core in range(2):
                    to = [x, y, z]
                    axis = (axis_first, axis_second)[core]
                    to[axis] = (to[axis] + by) % SIDE
                    pairs.append((flat_index(x, y, z, core), flat_index(*to, core)))
    return pairs


def ring(rows, axis_first, axis_second):
    pieces = [rows] + [lax.ppermute(rows, FLAT, shift(axis_first, axis_second, by)) for by in (1, -1, 2)]
    joined = jnp.zeros((len(pieces) * rows.shape[0], rows.shape[1]), rows.dtype)
    for i, piece in enumerate(pieces):
        joined = lax.dynamic_update_slice(joined, piece, (i * rows.shape[0], 0))
    return joined


def sibling(rows):
    return lax.ppermute(rows, "core", [(0, 1), (1, 0)])


SMEM = pl.BlockSpec(memory_space=pltpu.SMEM)
VMEM = pl.BlockSpec(memory_space=pltpu.VMEM)
ANY = pl.BlockSpec(memory_space=pl.ANY)


def iota(shape, axis):
    return lax.broadcasted_iota(jnp.int32, shape, axis)


def exact_dot(left, right):
    return jnp.dot(left.astype(jnp.bfloat16), right.astype(jnp.bfloat16), preferred_element_type=jnp.float32)


def sort_kernel(here_ref, packed_ref, pool_hbm, *refs):
    *pay_refs, tab_ref, pool_ref, sem = refs
    fetch = pltpu.make_async_copy(pool_hbm, pool_ref.at[pl.ds(0, ZERO)], sem)
    fetch.start()
    pool_ref[ZERO] = jnp.zeros((TILE, TILE), pool_ref.dtype)
    shape = (SLOTS, BLOCKS)
    my_x, my_y, my_z, my_core = (here_ref[i] for i in range(4))
    block, slot = iota(shape, 1), iota(shape, 0)
    y, z, low, core = block >> 4, (block >> 2) & 3, (block >> 1) & 1, block & 1

    def place(offset):
        offset = offset & 3
        return jnp.where(offset == 0, 0, jnp.where(offset == 3, 1, offset + 1))

    dy, dz = place(y - my_y), place(z - my_z)
    second, third = jnp.where(core == 0, dy, dz), jnp.where(core == 0, dz, dy)
    other = jnp.where(core == my_core, 0, 1)
    far_stage = jnp.where(second < 2, 2, 3) + other
    stage = jnp.where(third == 3, far_stage, jnp.where(third == 0, 0, 1))
    buf = jnp.where(third == 3, jnp.where(far_stage == 4, -16, 0), (jnp.where(third == 2, 2, 0) + other) * 32)
    lists, at, ids = [], [], []
    for r in range(RELS):
        packed = packed_ref[r]
        tile, cols = packed & 3, (packed >> 2) & 3
        ids.append((packed >> 4) & 31)
        stays = (third == 3) & ((tile >> 1) == (my_x >> 1))
        dx = place((cols >> 1) * 2 + low - my_x)
        at.append(jnp.where(stays, other * 32, buf) + (second * 4 + dx) * 2 + (cols & 1))
        live = slot < (packed >> 9)
        lists.append(jnp.where(live, jnp.where(stays, STAGES - 1, stage) * TPB + tile, STAGES * TPB))
    square = (RELS * TPB * SLOTS, RELS * TPB * SLOTS)
    row, col = iota(square, 0), iota(square, 1)
    same = (row >> 3) == (col >> 3)
    before = jnp.where(same & (col < row), 1.0, 0.0)
    whole = jnp.where(same, 1.0, 0.0)
    earlier = jnp.where(((col >> 3) < (row >> 3)) & ((col & 7) == 0), 1.0, 0.0)
    lanes = (BLOCKS, BLOCKS)
    upper = jnp.where(iota(lanes, 0) < iota(lanes, 1), 1.0, 0.0)
    ones = jnp.ones((BLOCKS, TILE), jnp.float32)
    pos, end = [], []
    for st in range(STAGES):
        member = jnp.concatenate(
            [jnp.where(lists[r] == st * TPB + t, 1.0, 0.0) for r in range(RELS) for t in range(TPB)], 0
        )
        row_sum = exact_dot(member, ones)
        above = exact_dot(before, row_sum)
        length = exact_dot(whole, row_sum)
        chunks = ((length.astype(jnp.int32) + (UNIT - 1)) >> 2).astype(jnp.float32)
        begin = exact_dot(earlier, chunks) + STARTS[st]
        end.append((begin + chunks).astype(jnp.int32))
        pos.append(member * ((begin * UNIT + above)[:, :BLOCKS] + exact_dot(member, upper)))

    out = jnp.zeros((PAY_ROWS, 2 * TILE), jnp.float32)
    for r in range(RELS):
        where = jnp.zeros(shape, jnp.float32)
        for st in range(STAGES):
            for t in range(TPB):
                first = (r * TPB + t) * SLOTS
                where = where + pos[st][first : first + SLOTS]
        where = jnp.where(lists[r] == STAGES * TPB, -1, where.astype(jnp.int32))
        high, low_part = where >> 7, where & 127
        weight = (ids[r] + (r * POOL - ZERO)).astype(jnp.float32)
        source = at[r].astype(jnp.float32)
        for k in range(SLOTS):
            left = jnp.where(iota((PAY_ROWS, BLOCKS), 0) == high[k : k + 1], 1.0, 0.0)
            hit = iota((TILE, BLOCKS), 0) == low_part[k : k + 1]
            right = jnp.concatenate(
                [jnp.where(hit, weight[k : k + 1], 0.0), jnp.where(hit, source[k : k + 1], 0.0)], 0
            )
            out = out + lax.dot_general(
                left.astype(jnp.bfloat16),
                right.astype(jnp.bfloat16),
                (((1,), (1,)), ((), ())),
                preferred_element_type=jnp.float32,
            )
    out = out.astype(jnp.int32)
    pay = ((out[:, :TILE] + ZERO) << 7) | out[:, TILE:]
    for ref, (first, last) in zip(pay_refs, PAY_SPANS, strict=True):
        ref[...] = pay[first:last]

    index = iota((TAB_ROWS, TILE), 0) * TILE + iota((TAB_ROWS, TILE), 1)
    table = jnp.zeros((TAB_ROWS, TILE), jnp.int32)
    for st in range(STAGES):
        tile = jnp.zeros((TAB_ROWS, TILE), jnp.int32)
        for g in range(RELS * TPB):
            tile = tile + jnp.where(index >= end[st][g * SLOTS : (g + 1) * SLOTS], 1, 0)
        inside = (index >= STARTS[st]) & (index < STARTS[st + 1])
        table = jnp.where(inside, jnp.minimum(tile, RELS * TPB - 1), table)
        total = end[st][-SLOTS:] - STARTS[st]
        table = jnp.where(index == (TAB_ROWS - 1) * TILE + st, total, table)
    tab_ref[...] = table
    fetch.wait()


def sort_slots(here, packed, pool):
    return pl.pallas_call(
        sort_kernel,
        out_shape=[
            *(jax.ShapeDtypeStruct((last - first, TILE), jnp.int32) for first, last in PAY_SPANS),
            jax.ShapeDtypeStruct((TAB_ROWS, TILE), jnp.int32),
            jax.ShapeDtypeStruct((ZERO + 1, TILE, TILE), pool.dtype),
        ],
        in_specs=[SMEM, VMEM, ANY],
        out_specs=[VMEM] * (STAGES + 2),
        scratch_shapes=[pltpu.SemaphoreType.DMA],
        compiler_params=pltpu.CompilerParams(vmem_limit_bytes=24 << 20),
        cost_estimate=pl.CostEstimate(flops=0, bytes_accessed=8 << 20, transcendentals=0),
        name="sort_slots",
    )(here, packed, pool)


def stage_kernel(st, count, *refs):
    refs = list(refs)
    pay, tab, pool = refs[:3]
    bufs = refs[3 : 3 + count]
    del refs[: 3 + count]
    copies = []
    if st == 0:
        total = refs.pop(0)
        total[...] = jnp.zeros_like(total)
    elif st < STAGES - 2:
        _, total, *refs = refs
    elif st == STAGES - 2:
        _, chan, transforms, total, theirs, *refs = refs
    else:
        before, chan, transforms, selfterm, mine, total, *refs = refs
        total[...] = before[...]
    if count > 1:
        rows, sems = refs
        at = 0
        for buf in bufs:
            copies.append((buf, rows.at[pl.ds(at, buf.shape[0])]))
            at += buf.shape[0]
        copies = [pltpu.make_async_copy(*copy, sems.at[i]) for i, copy in enumerate(copies)]
        for copy in copies:
            copy.start()
        for copy in copies:
            copy.wait()
    else:
        rows = bufs[0]

    def turn(i, _):
        for c in range(WIDE[st]):
            chunk = STARTS[st] + i * WIDE[st] + c
            left, right = [], []
            for u in range(UNIT):
                value = pay[(chunk >> 5) - PAY_SPANS[st][0], (chunk & 31) * UNIT + u]
                left.append(pool[value >> 7])
                right.append(rows[value & 127])
            total[tab[chunk >> 7, chunk & 127]] += jnp.dot(
                jnp.concatenate(left, 1), jnp.concatenate(right, 0), preferred_element_type=jnp.float32
            )
        return 0

    turns = (tab[TAB_ROWS - 1, st] + (WIDE[st] - 1)) >> (WIDE[st].bit_length() - 1)
    lax.fori_loop(0, turns, turn, 0)

    def final(tile):
        parts = [
            jnp.dot(total[r * TPB + tile].astype(jnp.bfloat16), transforms[r], preferred_element_type=jnp.float32)
            for r in range(RELS)
        ]
        return (parts[0] + parts[1]) + (parts[2] + parts[3])

    half = TPB // 2
    for u in range(half):
        if st == STAGES - 2:
            theirs[u] = final((1 - chan[0]) * half + u).astype(jnp.bfloat16)
        if st == STAGES - 1:
            mine[u] = final(chan[0] * half + u) + selfterm[u]


def run_stage(st, lists, pool, bufs, *more):
    args = [lists[st], lists[-1], pool, *bufs, *more]
    specs = [SMEM] * 2 + [VMEM] + [ANY if len(bufs) > 1 else VMEM] * len(bufs)
    specs += [VMEM, SMEM, VMEM, VMEM][: len(more)]
    wide = (RELS * TPB, TILE, TILE)
    half = (TPB // 2, TILE, TILE)
    out = [jax.ShapeDtypeStruct(wide, jnp.float32)]
    scratch, aliases = [], {}
    if st == STAGES - 1:
        out = [jax.ShapeDtypeStruct(half, jnp.float32)]
        scratch = [pltpu.VMEM(wide, jnp.float32)]
    elif st > 0:
        aliases = {3 + len(bufs): 0}
    if st == STAGES - 2:
        out.append(jax.ShapeDtypeStruct(half, jnp.bfloat16))
    if len(bufs) > 1:
        scratch.append(pltpu.VMEM((SIZES[st], TILE, TILE), jnp.bfloat16))
        scratch.append(pltpu.SemaphoreType.DMA((len(bufs),)))
    return pl.pallas_call(
        functools.partial(stage_kernel, st, len(bufs)),
        out_shape=out,
        in_specs=specs,
        out_specs=[VMEM] * len(out),
        scratch_shapes=scratch,
        input_output_aliases=aliases,
        compiler_params=pltpu.CompilerParams(vmem_limit_bytes=24 << 20),
        cost_estimate=pl.CostEstimate(flops=FLOPS[st], bytes_accessed=8 << 20, transcendentals=0),
        name=f"stage{st}",
    )(*args)


def shards(features, transforms, self_weight, tile_rows, tile_cols, tile_ids, tile_count, tile_pool):
    chan, xl = lax.axis_index("chan"), lax.axis_index("xl")
    own = features[0, 0]
    half_rows, width = own.shape
    here = jnp.stack(
        [chan * 2 + xl, lax.axis_index("y"), lax.axis_index("z"), lax.axis_index("core")]
    ).astype(jnp.int32)

    def by_slot(table):
        return table[:, 0].transpose(0, 2, 1)

    line = ring(own, 0, 0)
    selfterm = jnp.dot(own, self_weight, preferred_element_type=jnp.float32).reshape(-1, TILE, width)
    now = lax.dynamic_slice_in_dim(transforms, chan * RELS, RELS, 0)
    packed = by_slot(tile_rows) | (by_slot(tile_cols) << 2) | (by_slot(tile_ids) << 4)
    packed = packed | (tile_count[:, 0][:, None, :] << 9)
    line, packed, selfterm, now = lax.optimization_barrier((line, packed, selfterm, now))
    plane = ring(line, 1, 2)
    pool = tile_pool.reshape(RELS * POOL, TILE, TILE)
    *lists, pool = sort_slots(here, packed, pool)
    plane, lists, pool = lax.optimization_barrier((plane, lists, pool))
    plane = plane.reshape(-1, TILE, width)
    left = lax.ppermute(plane, FLAT, shift(2, 1, 1))
    right = lax.ppermute(plane, FLAT, shift(2, 1, -1))
    total = run_stage(0, lists, pool, [plane, sibling(plane)])[0]
    left, right, total = lax.optimization_barrier((left, right, total))
    half = plane.shape[0] // 2
    first = lax.ppermute(left[:half], FLAT, shift(2, 1, 1))
    second = lax.ppermute(right[half:], FLAT, shift(2, 1, -1))
    total = run_stage(1, lists, pool, [left, sibling(left), right, sibling(right)], total)[0]
    first, total = lax.optimization_barrier((first, total))
    other = sibling(first)
    total = run_stage(2, lists, pool, [first], total)[0]
    second, total = lax.optimization_barrier((second, total))
    last = sibling(second)
    total = run_stage(3, lists, pool, [other, second], total)[0]
    total, sent = run_stage(4, lists, pool, [last], total, here[:1] >> 1, now)
    got = lax.ppermute(sent, "chan", [(0, 1), (1, 0)])
    kept = run_stage(5, lists, pool, [first, second, other, last], total, here[:1] >> 1, now, selfterm)[0]
    updated = jax.nn.relu(kept + got.astype(jnp.float32)).astype(jnp.bfloat16)
    return updated.reshape(1, 1, half_rows, width)


def solution(mesh):
    fine = Mesh(mesh.devices.reshape(2, SIDE, SIDE, 2, 2), FLAT)
    blk = ("y", "z", "xl", "core")
    placed = (
        P(blk, "chan", None, None),
        P(),
        P(),
        P("chan", blk, None, None),
        P("chan", blk, None, None),
        P("chan", blk, None, None),
        P("chan", blk, None),
        P("chan", blk, None, None, None),
    )
    return jax.shard_map(
        shards, mesh=fine, in_specs=placed, out_specs=P(blk, "chan", None, None), check_vma=False
    )
```

```python
import functools

import jax
import jax.numpy as jnp
from jax import lax
from jax.experimental import pallas as pl
from jax.experimental.pallas import tpu as pltpu
from jax.sharding import Mesh, PartitionSpec as P

SIDE = 4
TILE = 128
RELS = 4
POOL = 32
TPB = 4
SLOTS = 8
BLOCKS = 64
ZERO = RELS * POOL
UNIT = 4
WIDE = (16, 16, 16, 8, 16, 8)
SIZES = (64, 128, 16, 32, 16, 64)
STAGES = len(SIZES)
FLOPS = (4 << 30, 8 << 30, 1 << 30, 2 << 30, 1 << 30, 2 << 30)


def most_chunks(st):
    most = (RELS * 2 * SIZES[st] + (UNIT - 1) * RELS * TPB) // UNIT
    return -(-most // WIDE[st]) * WIDE[st]


STARTS = tuple(sum(most_chunks(i) for i in range(st)) for st in range(STAGES + 1))
PAY_ROWS = -(-STARTS[-1] * UNIT // (8 * TILE)) * 8
PAY_SPANS = tuple((STARTS[st] * UNIT // TILE, -(-STARTS[st + 1] * UNIT // TILE)) for st in range(STAGES))
TAB_ROWS = 8
GROUPS = STAGES * RELS * TPB

FLAT = ("chan", "y", "z", "xl", "core")


def flat_index(x, y, z, core):
    return ((((x // 2) * SIDE + y) * SIDE + z) * 2 + x % 2) * 2 + core


def shift(axis_first, axis_second, by):
    pairs = []
    for x in range(SIDE):
        for y in range(SIDE):
            for z in range(SIDE):
                for core in range(2):
                    to = [x, y, z]
                    axis = (axis_first, axis_second)[core]
                    to[axis] = (to[axis] + by) % SIDE
                    pairs.append((flat_index(x, y, z, core), flat_index(*to, core)))
    return pairs


def ring(rows, axis_first, axis_second):
    pieces = [rows] + [lax.ppermute(rows, FLAT, shift(axis_first, axis_second, by)) for by in (1, -1, 2)]
    joined = jnp.zeros((len(pieces) * rows.shape[0], rows.shape[1]), rows.dtype)
    for i, piece in enumerate(pieces):
        joined = lax.dynamic_update_slice(joined, piece, (i * rows.shape[0], 0))
    return joined


def sibling(rows):
    return lax.ppermute(rows, "core", [(0, 1), (1, 0)])


SMEM = pl.BlockSpec(memory_space=pltpu.SMEM)
VMEM = pl.BlockSpec(memory_space=pltpu.VMEM)
ANY = pl.BlockSpec(memory_space=pl.ANY)


def iota(shape, axis):
    return lax.broadcasted_iota(jnp.int32, shape, axis)


def exact_dot(left, right):
    return jnp.dot(left.astype(jnp.bfloat16), right.astype(jnp.bfloat16), preferred_element_type=jnp.float32)


def sort_kernel(here_ref, packed_ref, pool_hbm, *refs):
    *pay_refs, tab_ref, pool_ref, sem = refs
    fetch = pltpu.make_async_copy(pool_hbm, pool_ref.at[pl.ds(0, ZERO)], sem)
    fetch.start()
    pool_ref[ZERO] = jnp.zeros((TILE, TILE), pool_ref.dtype)
    shape = (SLOTS, BLOCKS)
    my_x, my_y, my_z, my_core = (here_ref[i] for i in range(4))
    block, slot = iota(shape, 1), iota(shape, 0)
    y, z, low, core = block >> 4, (block >> 2) & 3, (block >> 1) & 1, block & 1

    def place(offset):
        offset = offset & 3
        return jnp.where(offset == 0, 0, jnp.where(offset == 3, 1, offset + 1))

    dy, dz = place(y - my_y), place(z - my_z)
    second, third = jnp.where(core == 0, dy, dz), jnp.where(core == 0, dz, dy)
    other = jnp.where(core == my_core, 0, 1)
    far_stage = jnp.where(second < 2, 2, 3) + other
    stage = jnp.where(third == 3, far_stage, jnp.where(third == 0, 0, 1))
    buf = jnp.where(third == 3, jnp.where(far_stage == 4, -16, 0), (jnp.where(third == 2, 2, 0) + other) * 32)
    lists, at, ids = [], [], []
    for r in range(RELS):
        packed = packed_ref[r]
        tile, cols = packed & 3, (packed >> 2) & 3
        ids.append((packed >> 4) & 31)
        stays = (third == 3) & ((tile >> 1) == (my_x >> 1))
        dx = place((cols >> 1) * 2 + low - my_x)
        at.append(jnp.where(stays, other * 32, buf) + (second * 4 + dx) * 2 + (cols & 1))
        live = slot < (packed >> 9)
        lists.append(jnp.where(live, jnp.where(stays, STAGES - 1, stage) * TPB + tile, STAGES * TPB))
    square = (RELS * TPB * SLOTS, RELS * TPB * SLOTS)
    row, col = iota(square, 0), iota(square, 1)
    same = (row >> 3) == (col >> 3)
    before = jnp.where(same & (col < row), 1.0, 0.0)
    whole = jnp.where(same, 1.0, 0.0)
    earlier = jnp.where(((col >> 3) < (row >> 3)) & ((col & 7) == 0), 1.0, 0.0)
    lanes = (BLOCKS, BLOCKS)
    upper = jnp.where(iota(lanes, 0) < iota(lanes, 1), 1.0, 0.0)
    ones = jnp.ones((BLOCKS, TILE), jnp.float32)
    pos, end = [], []
    for st in range(STAGES):
        member = jnp.concatenate(
            [jnp.where(lists[r] == st * TPB + t, 1.0, 0.0) for r in range(RELS) for t in range(TPB)], 0
        )
        row_sum = exact_dot(member, ones)
        above = exact_dot(before, row_sum)
        length = exact_dot(whole, row_sum)
        chunks = ((length.astype(jnp.int32) + (UNIT - 1)) >> 2).astype(jnp.float32)
        begin = exact_dot(earlier, chunks) + STARTS[st]
        end.append((begin + chunks).astype(jnp.int32))
        pos.append(member * ((begin * UNIT + above)[:, :BLOCKS] + exact_dot(member, upper)))

    out = jnp.zeros((PAY_ROWS, 2 * TILE), jnp.float32)
    for r in range(RELS):
        where = jnp.zeros(shape, jnp.float32)
        for st in range(STAGES):
            for t in range(TPB):
                first = (r * TPB + t) * SLOTS
                where = where + pos[st][first : first + SLOTS]
        where = jnp.where(lists[r] == STAGES * TPB, -1, where.astype(jnp.int32))
        high, low_part = where >> 7, where & 127
        weight = (ids[r] + (r * POOL - ZERO)).astype(jnp.float32)
        source = at[r].astype(jnp.float32)
        for k in range(SLOTS):
            left = jnp.where(iota((PAY_ROWS, BLOCKS), 0) == high[k : k + 1], 1.0, 0.0)
            hit = iota((TILE, BLOCKS), 0) == low_part[k : k + 1]
            right = jnp.concatenate(
                [jnp.where(hit, weight[k : k + 1], 0.0), jnp.where(hit, source[k : k + 1], 0.0)], 0
            )
            out = out + lax.dot_general(
                left.astype(jnp.bfloat16),
                right.astype(jnp.bfloat16),
                (((1,), (1,)), ((), ())),
                preferred_element_type=jnp.float32,
            )
    out = out.astype(jnp.int32)
    pay = ((out[:, :TILE] + ZERO) << 7) | out[:, TILE:]
    for ref, (first, last) in zip(pay_refs, PAY_SPANS, strict=True):
        ref[...] = pay[first:last]

    index = iota((TAB_ROWS, TILE), 0) * TILE + iota((TAB_ROWS, TILE), 1)
    table = jnp.zeros((TAB_ROWS, TILE), jnp.int32)
    for st in range(STAGES):
        tile = jnp.zeros((TAB_ROWS, TILE), jnp.int32)
        for g in range(RELS * TPB):
            tile = tile + jnp.where(index >= end[st][g * SLOTS : (g + 1) * SLOTS], 1, 0)
        inside = (index >= STARTS[st]) & (index < STARTS[st + 1])
        table = jnp.where(inside, jnp.minimum(tile, RELS * TPB - 1), table)
        total = end[st][-SLOTS:] - STARTS[st]
        table = jnp.where(index == (TAB_ROWS - 1) * TILE + st, total, table)
    tab_ref[...] = table
    fetch.wait()


def sort_slots(here, packed, pool):
    return pl.pallas_call(
        sort_kernel,
        out_shape=[
            *(jax.ShapeDtypeStruct((last - first, TILE), jnp.int32) for first, last in PAY_SPANS),
            jax.ShapeDtypeStruct((TAB_ROWS, TILE), jnp.int32),
            jax.ShapeDtypeStruct((ZERO + 1, TILE, TILE), pool.dtype),
        ],
        in_specs=[SMEM, VMEM, ANY],
        out_specs=[VMEM] * (STAGES + 2),
        scratch_shapes=[pltpu.SemaphoreType.DMA],
        compiler_params=pltpu.CompilerParams(vmem_limit_bytes=24 << 20),
        cost_estimate=pl.CostEstimate(flops=0, bytes_accessed=8 << 20, transcendentals=0),
        name="sort_slots",
    )(here, packed, pool)


def stage_kernel(st, count, *refs):
    refs = list(refs)
    pay, tab, pool = refs[:3]
    bufs = refs[3 : 3 + count]
    del refs[: 3 + count]
    copies = []
    if st == 0:
        total = refs.pop(0)
        total[...] = jnp.zeros_like(total)
    elif st < STAGES - 2:
        _, total, *refs = refs
    elif st == STAGES - 2:
        _, chan, transforms, total, theirs, *refs = refs
    else:
        before, chan, transforms, selfterm, mine, total, *refs = refs
        total[...] = before[...]
    if count > 1:
        rows, sems = refs
        at = 0
        for buf in bufs:
            copies.append((buf, rows.at[pl.ds(at, buf.shape[0])]))
            at += buf.shape[0]
        copies = [pltpu.make_async_copy(*copy, sems.at[i]) for i, copy in enumerate(copies)]
        for copy in copies:
            copy.start()
        for copy in copies:
            copy.wait()
    else:
        rows = bufs[0]

    def turn(i, _):
        for c in range(WIDE[st]):
            chunk = STARTS[st] + i * WIDE[st] + c
            left, right = [], []
            for u in range(UNIT):
                value = pay[(chunk >> 5) - PAY_SPANS[st][0], (chunk & 31) * UNIT + u]
                left.append(pool[value >> 7])
                right.append(rows[value & 127])
            total[tab[chunk >> 7, chunk & 127]] += jnp.dot(
                jnp.concatenate(left, 1), jnp.concatenate(right, 0), preferred_element_type=jnp.float32
            )
        return 0

    turns = (tab[TAB_ROWS - 1, st] + (WIDE[st] - 1)) >> (WIDE[st].bit_length() - 1)
    lax.fori_loop(0, turns, turn, 0)

    def final(tile):
        parts = [
            jnp.dot(total[r * TPB + tile].astype(jnp.bfloat16), transforms[r], preferred_element_type=jnp.float32)
            for r in range(RELS)
        ]
        return (parts[0] + parts[1]) + (parts[2] + parts[3])

    half = TPB // 2
    for u in range(half):
        if st == STAGES - 2:
            theirs[u] = final((1 - chan[0]) * half + u).astype(jnp.bfloat16)
        if st == STAGES - 1:
            mine[u] = final(chan[0] * half + u) + selfterm[u]


def run_stage(st, lists, pool, bufs, *more):
    args = [lists[st], lists[-1], pool, *bufs, *more]
    specs = [SMEM] * 2 + [VMEM] + [ANY if len(bufs) > 1 else VMEM] * len(bufs)
    specs += [VMEM, SMEM, VMEM, VMEM][: len(more)]
    wide = (RELS * TPB, TILE, TILE)
    half = (TPB // 2, TILE, TILE)
    out = [jax.ShapeDtypeStruct(wide, jnp.float32)]
    scratch, aliases = [], {}
    if st == STAGES - 1:
        out = [jax.ShapeDtypeStruct(half, jnp.float32)]
        scratch = [pltpu.VMEM(wide, jnp.float32)]
    elif st > 0:
        aliases = {3 + len(bufs): 0}
    if st == STAGES - 2:
        out.append(jax.ShapeDtypeStruct(half, jnp.bfloat16))
    if len(bufs) > 1:
        scratch.append(pltpu.VMEM((SIZES[st], TILE, TILE), jnp.bfloat16))
        scratch.append(pltpu.SemaphoreType.DMA((len(bufs),)))
    return pl.pallas_call(
        functools.partial(stage_kernel, st, len(bufs)),
        out_shape=out,
        in_specs=specs,
        out_specs=[VMEM] * len(out),
        scratch_shapes=scratch,
        input_output_aliases=aliases,
        compiler_params=pltpu.CompilerParams(vmem_limit_bytes=24 << 20),
        cost_estimate=pl.CostEstimate(flops=FLOPS[st], bytes_accessed=8 << 20, transcendentals=0),
        name=f"stage{st}",
    )(*args)


def shards(features, transforms, self_weight, tile_rows, tile_cols, tile_ids, tile_count, tile_pool):
    chan, xl = lax.axis_index("chan"), lax.axis_index("xl")
    own = features[0, 0]
    half_rows, width = own.shape
    here = jnp.stack(
        [chan * 2 + xl, lax.axis_index("y"), lax.axis_index("z"), lax.axis_index("core")]
    ).astype(jnp.int32)

    def by_slot(table):
        return table[:, 0].transpose(0, 2, 1)

    line = ring(own, 0, 0)
    selfterm = jnp.dot(own, self_weight, preferred_element_type=jnp.float32).reshape(-1, TILE, width)
    now = lax.dynamic_slice_in_dim(transforms, chan * RELS, RELS, 0)
    packed = by_slot(tile_rows) | (by_slot(tile_cols) << 2) | (by_slot(tile_ids) << 4)
    packed = packed | (tile_count[:, 0][:, None, :] << 9)
    line, packed, selfterm, now = lax.optimization_barrier((line, packed, selfterm, now))
    plane = ring(line, 1, 2)
    pool = tile_pool.reshape(RELS * POOL, TILE, TILE)
    *lists, pool = sort_slots(here, packed, pool)
    plane, lists, pool = lax.optimization_barrier((plane, lists, pool))
    plane = plane.reshape(-1, TILE, width)
    left = lax.ppermute(plane, FLAT, shift(2, 1, 1))
    right = lax.ppermute(plane, FLAT, shift(2, 1, -1))
    total = run_stage(0, lists, pool, [plane, sibling(plane)])[0]
    left, right, total = lax.optimization_barrier((left, right, total))
    half = plane.shape[0] // 2
    first = lax.ppermute(left[:half], FLAT, shift(2, 1, 1))
    second = lax.ppermute(right[half:], FLAT, shift(2, 1, -1))
    total = run_stage(1, lists, pool, [left, sibling(left), right, sibling(right)], total)[0]
    first, total = lax.optimization_barrier((first, total))
    other = sibling(first)
    total = run_stage(2, lists, pool, [first], total)[0]
    second, total = lax.optimization_barrier((second, total))
    last = sibling(second)
    total = run_stage(3, lists, pool, [other, second], total)[0]
    total, sent = run_stage(4, lists, pool, [last], total, here[:1] >> 1, now)
    got = lax.ppermute(sent, "chan", [(0, 1), (1, 0)])
    kept = run_stage(5, lists, pool, [first, second, other, last], total, here[:1] >> 1, now, selfterm)[0]
    updated = jax.nn.relu(kept + got.astype(jnp.float32)).astype(jnp.bfloat16)
    return updated.reshape(1, 1, half_rows, width)


def solution(mesh):
    fine = Mesh(mesh.devices.reshape(2, SIDE, SIDE, 2, 2), FLAT)
    blk = ("y", "z", "xl", "core")
    placed = (
        P(blk, "chan", None, None),
        P(),
        P(),
        P("chan", blk, None, None),
        P("chan", blk, None, None),
        P("chan", blk, None, None),
        P("chan", blk, None),
        P("chan", blk, None, None, None),
    )
    return jax.shard_map(
        shards, mesh=fine, in_specs=placed, out_specs=P(blk, "chan", None, None), check_vma=False
    )
```
